32 devices in a mesh: groups: 2 (over y), seq: 16 (over z, x, core).
Axes of the slice: x: 2, y: 2, z: 4, core: 2. Of those that a mesh axis runs over, the one named last changes fastest.
Arguments:
- streams: bfloat16 [3, 4096, 2048], P(None, ('groups', 'seq')), parts along dimension 1, may hold values from -6 to 6
- short_kernel: float32 [3, 3, 2048], replicated, may hold values from -3.5 to 3.5
- filters: float32 [2, 32, 384], replicated, may hold values from -0.3125 to 0.3125
- cotangent: bfloat16 [4096, 2048], P(('groups', 'seq')), parts along dimension 0, may hold values from -6 to 6
Outputs:
- output: bfloat16 [4096, 2048], P(('groups', 'seq')), parts along dimension 0
- grad_streams: bfloat16 [3, 4096, 2048], P(None, ('groups', 'seq')), parts along dimension 1
- grad_short: float32 [6, 3, 2048], P('groups'), parts along dimension 0
- grad_filters: float32 [4, 32, 384], P('groups'), parts along dimension 0
The draws below stay inside these ranges and needn't reach their ends.
There are 2 independent parts, one for each index of `groups`. The reference program is written for one: setup_inputs(seed, part) draws one part's arguments, and reference() takes and returns one part's arrays. A program takes and returns all parts, laid end to end along the dimension named above; an argument that names none is the same for every part. Nothing has to cross between parts.
All inputs are finite; a program needn't handle non-finite values.
Results may differ from the reference program's by a relative error of at most 0.0081.
Values may be sent and summed in bfloat16 or wider, within the bound.
A program may use at most 128 MiB of HBM per device.

```python
import jax
import jax.numpy as jnp
from jax import lax

D = 2048
HEAD = 64
HEADS = 32
TOK_DEV = 128
SPAN = 3
FLEN = 384
TOKENS = 2048


def steps_of(rng, extent, split, low, top_value):
    loudness = 1.0
    for position, blocks in split:
        steps = jax.random.uniform(jax.random.fold_in(jax.random.fold_in(rng, 6), position), (blocks,), jnp.float32, low / len(split), top_value / len(split))
        loudness = loudness * jnp.repeat(jnp.exp(steps), extent[position] // blocks).reshape((-1,) + (1,) * (len(extent) - 1 - position))
    return loudness


def gaussian(stream_key, extent, scale, reach, split=(), kind=jnp.bfloat16):
    result = jax.random.normal(stream_key, extent, jnp.float32) * scale
    if len(split) > 0:
        result = steps_of(stream_key, extent, split, -0.22, 0.18) * result
    return jnp.clip(result, min=-reach, max=reach).astype(kind)


def setup_inputs(seed: int = 0, part: int = 0) -> dict:
    arg_keys = jax.random.split(jax.random.key(seed), 5)
    part_keys = jax.random.split(jax.random.fold_in(arg_keys[4], part), 5)
    streams = gaussian(part_keys[0], (3, TOKENS, D), 1.0, 6.0, ((1, 16),))
    short_kernel = gaussian(arg_keys[1], (3, 3, D), 3 ** -0.5, 3.5, (), jnp.float32)
    filters = gaussian(arg_keys[2], (2, HEADS, FLEN), FLEN ** -0.5, 0.3125, (), jnp.float32)
    cotangent = gaussian(part_keys[3], (TOKENS, D), 1.0, 6.0, ((0, 16),))
    return {"streams": streams, "short_kernel": short_kernel, "filters": filters, "cotangent": cotangent}


def toeplitz_stack(row, block_rows, span_blocks):
    heads_count = row.shape[0]
    padded = jnp.pad(row, ((0, 0), (block_rows, block_rows)))
    matrices = []
    for distance in range(span_blocks + 1):
        segment = padded[:, distance * block_rows + 1:distance * block_rows + 2 * block_rows][:, ::-1]
        tiled = jnp.tile(segment, (1, block_rows))
        window = tiled[:, block_rows - 1:block_rows - 1 + block_rows * (2 * block_rows - 2)]
        matrices.append(window.reshape(heads_count, block_rows, 2 * block_rows - 2)[:, :, :block_rows])
    return jnp.stack(matrices)

def skew_sum(scores, block_rows):
    heads_count, row_count, col_count = scores.shape
    padded = jnp.pad(scores, ((0, 0), (0, 0), (0, block_rows)))
    flat = padded.reshape(heads_count, row_count * (col_count + block_rows))
    window = flat[:, :row_count * (col_count + block_rows - 1)]
    return window.reshape(heads_count, row_count, col_count + block_rows - 1).sum(axis=1)

def reference(streams, short_kernel, filters, cotangent):
    count = TOKENS // TOK_DEV
    f32 = jnp.float32
    widened = jnp.pad(streams.astype(f32), ((0, 0), (2, 0), (0, 0)))
    kernel = short_kernel
    short = (kernel[:, 0:1] * widened[:, 2:] + kernel[:, 1:2] * widened[:, 1:-1] + kernel[:, 2:3] * widened[:, :-2]).astype(jnp.bfloat16)
    gate_first, gate_second, values = (short[0], short[1], short[2])
    taps = filters.astype(jnp.bfloat16)
    toeplitz_one = toeplitz_stack(taps[0], TOK_DEV, SPAN).astype(f32)
    toeplitz_two = toeplitz_stack(taps[1], TOK_DEV, SPAN).astype(f32)
    zeros_blocks = jnp.zeros((SPAN, TOK_DEV, HEADS, HEAD), f32)

    def earlier_padded(source):
        blocks = source.astype(f32).reshape(count, TOK_DEV, HEADS, HEAD)
        return jnp.concatenate([zeros_blocks, blocks], axis=0)

    def forward_conv(source, matrices):
        padded = earlier_padded(source)

        def single(index_block):
            stacked = lax.dynamic_slice_in_dim(padded, index_block, SPAN + 1, 0)[::-1]
            return jnp.einsum('dhrs,dshe->rhe', matrices, stacked)
        return lax.map(single, jnp.arange(count, dtype=jnp.int32)).reshape(TOKENS, D)

    def adjoint_conv(source, matrices):
        blocks = source.astype(f32).reshape(count, TOK_DEV, HEADS, HEAD)
        padded = jnp.concatenate([blocks, zeros_blocks], axis=0)

        def single(index_block):
            stacked = lax.dynamic_slice_in_dim(padded, index_block, SPAN + 1, 0)
            return jnp.einsum('dhrs,drhe->she', matrices, stacked)
        return lax.map(single, jnp.arange(count, dtype=jnp.int32)).reshape(TOKENS, D)

    def filter_grad(grad_source, source):
        padded = earlier_padded(source)
        grad_blocks = grad_source.astype(f32).reshape(count, TOK_DEV, HEADS, HEAD)

        def single(index_block):
            stacked = lax.dynamic_slice_in_dim(padded, index_block, SPAN + 1, 0)[::-1][:, ::-1]
            scores = jnp.einsum('rhe,dshe->hrds', grad_blocks[index_block], stacked)
            scores = scores.reshape(HEADS, TOK_DEV, (SPAN + 1) * TOK_DEV)
            return skew_sum(scores, TOK_DEV)
        total = lax.map(single, jnp.arange(count, dtype=jnp.int32)).sum(axis=0)
        return total[:, TOK_DEV - 1:TOK_DEV - 1 + FLEN]
    conv_one = forward_conv(values, toeplitz_one)
    inner = (gate_first.astype(f32) * conv_one).astype(jnp.bfloat16)
    conv_two = forward_conv(inner, toeplitz_two)
    output = (gate_second.astype(f32) * conv_two).astype(jnp.bfloat16)
    grad_out = cotangent.astype(f32)
    grad_second = grad_out * conv_two
    grad_conv_two = (grad_out * gate_second.astype(f32)).astype(jnp.bfloat16)
    grad_inner = adjoint_conv(grad_conv_two, toeplitz_two)
    grad_first = grad_inner * conv_one
    grad_conv_one = (grad_inner * gate_first.astype(f32)).astype(jnp.bfloat16)
    grad_values = adjoint_conv(grad_conv_one, toeplitz_one)
    stacked_grads = jnp.stack([grad_first, grad_second, grad_values])
    after = jnp.pad(stacked_grads, ((0, 0), (0, 2), (0, 0)))
    grad_streams = (kernel[:, 0:1] * after[:, :-2] + kernel[:, 1:2] * after[:, 1:-1] + kernel[:, 2:3] * after[:, 2:]).astype(jnp.bfloat16)
    kernel_terms = jnp.stack([lax.optimization_barrier(jnp.sum(stacked_grads * widened[:, 2:], axis=1)), lax.optimization_barrier(jnp.sum(stacked_grads * widened[:, 1:-1], axis=1)), lax.optimization_barrier(jnp.sum(stacked_grads * widened[:, :-2], axis=1))], axis=1)
    grad_short = kernel_terms / jnp.sqrt(jnp.float32(TOKENS))
    filter_one = filter_grad(grad_conv_one, values)
    filter_two = filter_grad(grad_conv_two, inner)
    grad_filters = jnp.stack([filter_one, filter_two]) / jnp.sqrt(jnp.float32(TOKENS * HEAD))
    return (output, grad_streams, grad_short, grad_filters)
```

```python
import functools

import jax
import jax.numpy as jnp
from jax import lax
from jax.experimental import pallas as pl
from jax.experimental.pallas import tpu as pltpu
from jax.sharding import PartitionSpec as P


def shifted(value, axis, by):
    size = lax.axis_size(axis)
    pairs = [(i, i + by) for i in range(size) if 0 <= i + by < size]
    return lax.ppermute(value, axis, pairs)


def band_matrix(row, block_rows, span_blocks):
    heads_count = row.shape[0]
    cols = (span_blocks + 1) * block_rows
    length = cols + block_rows - 1
    padded = jnp.pad(row, ((0, 0), (block_rows - 1, block_rows)))
    mirrored = padded[:, ::-1]
    tiled = jnp.tile(mirrored, (1, block_rows))
    window = tiled[:, block_rows - 1 : block_rows - 1 + block_rows * (length - 1)]
    return window.reshape(heads_count, block_rows, length - 1)[:, :, :cols]


def skew_sum(scores, block_rows):
    heads_count, row_count, col_count = scores.shape
    padded = jnp.pad(scores, ((0, 0), (0, 0), (0, block_rows)))
    flat = padded.reshape(heads_count, row_count * (col_count + block_rows))
    window = flat[:, : row_count * (col_count + block_rows - 1)]
    return window.reshape(heads_count, row_count, col_count + block_rows - 1).sum(axis=1)


def to_heads(blocks, heads_count):
    depth, block_rows, channels = blocks.shape
    merged = blocks.reshape(depth * block_rows, heads_count, channels // heads_count)
    return merged.transpose(1, 2, 0)


def from_heads(result):
    heads_count, head_size, row_count = result.shape
    return result.transpose(2, 0, 1).reshape(row_count, heads_count * head_size)


def earlier_blocks(source, span_blocks):
    blocks = [source]
    current = source
    for distance in range(1, span_blocks + 1):
        current = shifted(current, "seq", 1)
        blocks.append(current)
    return jnp.stack(blocks)


def later_blocks(source, span_blocks):
    blocks = [source]
    current = source
    for distance in range(1, span_blocks + 1):
        current = shifted(current, "seq", -1)
        blocks.append(current)
    return jnp.stack(blocks)


def apply_forward(band, stacked, heads_count):
    ordered = to_heads(stacked[::-1], heads_count)
    result = jnp.einsum("hej,hrj->her", ordered, band, preferred_element_type=jnp.float32)
    return from_heads(result)


def apply_adjoint(band, stacked, heads_count):
    depth, block_rows, channels = stacked.shape
    head_size = channels // heads_count
    ordered = stacked[::-1].reshape(depth, block_rows, heads_count, head_size)
    pieces = ordered.transpose(2, 3, 1, 0).reshape(heads_count, head_size, block_rows * depth)
    matrix = band.reshape(heads_count, block_rows * depth, block_rows)
    result = jnp.einsum("hek,hks->hes", pieces, matrix, preferred_element_type=jnp.float32)
    return from_heads(result)


def filter_terms(grad_source, stacked, heads_count, filt_len):
    block_rows = stacked.shape[1]
    flipped = to_heads(stacked[:, ::-1], heads_count)
    own_grad = to_heads(grad_source[None], heads_count)
    scores = jnp.einsum("her,hej->hrj", own_grad, flipped, preferred_element_type=jnp.float32)
    summed = skew_sum(scores, block_rows)
    return summed[:, block_rows - 1 : block_rows - 1 + filt_len]


def on_device(streams, short_kernel, filters, cotangent):
    f32 = jnp.float32
    block_rows = streams.shape[1]
    heads_count = filters.shape[1]
    filt_len = filters.shape[2]
    span_blocks = filt_len // block_rows
    head_size = streams.shape[2] // heads_count
    total_tokens = block_rows * lax.axis_size("seq")
    rim_rows = shifted(streams[:, block_rows - 2 :, :], "seq", 1)
    widened = jnp.concatenate([rim_rows, streams], axis=1).astype(f32)
    short = (
        short_kernel[:, 0:1] * widened[:, 2:]
        + short_kernel[:, 1:2] * widened[:, 1:-1]
        + short_kernel[:, 2:3] * widened[:, :-2]
    ).astype(jnp.bfloat16)
    gate_first, gate_second, values = (short[0], short[1], short[2])
    taps = filters.astype(jnp.bfloat16)
    band_one = band_matrix(taps[0], block_rows, span_blocks)
    band_two = band_matrix(taps[1], block_rows, span_blocks)
    earlier_one = earlier_blocks(values, span_blocks)
    conv_one = apply_forward(band_one, earlier_one, heads_count)
    inner = (gate_first.astype(f32) * conv_one).astype(jnp.bfloat16)
    earlier_two = earlier_blocks(inner, span_blocks)
    conv_two = apply_forward(band_two, earlier_two, heads_count)
    output = (gate_second.astype(f32) * conv_two).astype(jnp.bfloat16)
    grad_out = cotangent.astype(f32)
    grad_second = grad_out * conv_two
    grad_conv_two = (grad_out * gate_second.astype(f32)).astype(jnp.bfloat16)
    later_two = later_blocks(grad_conv_two, span_blocks)
    grad_inner = apply_adjoint(band_two, later_two, heads_count)
    grad_first = grad_inner * conv_one
    grad_conv_one = (grad_inner * gate_first.astype(f32)).astype(jnp.bfloat16)
    later_one = later_blocks(grad_conv_one, span_blocks)
    grad_values = apply_adjoint(band_one, later_one, heads_count)
    filter_one = filter_terms(grad_conv_one, earlier_one, heads_count, filt_len)
    filter_two = filter_terms(grad_conv_two, earlier_two, heads_count, filt_len)
    stacked_grads = jnp.stack([grad_first, grad_second, grad_values])
    next_rows = shifted(stacked_grads[:, :2, :].astype(jnp.bfloat16), "seq", -1).astype(jnp.float32)
    after = jnp.concatenate([stacked_grads, next_rows], axis=1)
    grad_streams = (
        short_kernel[:, 0:1] * after[:, :block_rows]
        + short_kernel[:, 1:2] * after[:, 1 : block_rows + 1]
        + short_kernel[:, 2:3] * after[:, 2:]
    ).astype(jnp.bfloat16)
    kernel_terms = jnp.stack(
        [
            jnp.sum(stacked_grads * widened[:, 2:], axis=1),
            jnp.sum(stacked_grads * widened[:, 1:-1], axis=1),
            jnp.sum(stacked_grads * widened[:, :-2], axis=1),
        ],
        axis=1,
    )
    kernel_total, filter_total = lax.psum(
        (kernel_terms, jnp.stack([filter_one, filter_two])), "seq"
    )
    grad_short = kernel_total / jnp.sqrt(jnp.float32(total_tokens))
    grad_filters = filter_total / jnp.sqrt(jnp.float32(total_tokens * head_size))
    return (output, grad_streams, grad_short, grad_filters)


def pair_select(stacked, rows, head_size):
    lane = lax.broadcasted_iota(jnp.int32, (rows, 2 * head_size), 1)
    return jnp.where(lane < head_size, stacked[:rows], stacked[rows:])


def local_kernel(rows, filt_len, x_ref, sk_ref, fwd_ref, adj_ref,
                 y_ref, gshort_ref, gfilt_ref,
                 bands, adjs, vbuf, ibuf, gbuf, hbuf, first, second, conv, gs):
    f32, bf16 = jnp.float32, jnp.bfloat16
    tokens, chans = x_ref.shape[1], x_ref.shape[2]
    head_size = chans // 2
    count = tokens // rows
    window = filt_len + rows
    for k in range(2):
        for h in range(2):
            part = pl.ds(h * rows, rows)
            for src, dst in ((fwd_ref, bands), (adj_ref, adjs)):
                line = jnp.broadcast_to(src[pl.ds(2 * k + h, 1), :], (rows, window))
                dst[k, part, :] = pltpu.roll(line, 0, 1, stride=1, stride_axis=0).astype(bf16)
    blank = jnp.zeros((filt_len, chans), bf16)
    vbuf[pl.ds(0, filt_len), :] = blank
    ibuf[pl.ds(0, filt_len), :] = blank
    gbuf[pl.ds(tokens, filt_len), :] = blank
    hbuf[pl.ds(tokens, filt_len), :] = blank

    def delayed(c, n):
        x = x_ref[c, pl.ds(n * rows, rows), :].astype(f32)
        if n == 0:
            head = jnp.zeros((16, chans), f32)
        else:
            head = x_ref[c, pl.ds(n * rows - 16, 16), :].astype(f32)
        wide = jnp.concatenate([head, x], axis=0)
        return x, wide[15:15 + rows], wide[14:14 + rows]

    for n in range(count):
        here = pl.ds(n * rows, rows)
        short = []
        for c in range(3):
            x0, x1, x2 = delayed(c, n)
            short.append((sk_ref[c, 0:1] * x0 + sk_ref[c, 1:2] * x1 + sk_ref[c, 2:3] * x2).astype(bf16))
        first[here, :] = short[0]
        second[here, :] = short[1]
        vbuf[pl.ds(filt_len + n * rows, rows), :] = short[2]
        gbuf[here, :] = (x_ref[3, here, :].astype(f32) * short[1].astype(f32)).astype(bf16)

    def long(mat, src, n):
        stacked = jnp.dot(mat, src[pl.ds(n * rows, window), :], preferred_element_type=f32)
        return pair_select(stacked, rows, head_size)

    for n in range(count):
        here = pl.ds(n * rows, rows)
        gate = first[here, :].astype(f32)
        one = long(bands[0], vbuf, n)
        ibuf[pl.ds(filt_len + n * rows, rows), :] = (gate * one).astype(bf16)
        back = long(adjs[1], gbuf, n)
        gs[0, here, :] = back * one
        hbuf[here, :] = (back * gate).astype(bf16)

    flip_r = lax.broadcasted_iota(jnp.int32, (rows, rows), 0)
    flip_c = lax.broadcasted_iota(jnp.int32, (rows, rows), 1)
    flip = (flip_r + flip_c == rows - 1).astype(f32).astype(bf16)
    lane = lax.broadcasted_iota(jnp.int32, (rows, chans), 1)

    def scores(grad, src, n):
        turned = jnp.dot(flip, grad[pl.ds(n * rows, rows), :], preferred_element_type=f32)
        low = jnp.where(lane < head_size, turned, 0.0).astype(bf16)
        high = jnp.where(lane < head_size, 0.0, turned).astype(bf16)
        return lax.dot_general(
            jnp.concatenate([low, high], axis=0), src[pl.ds(n * rows, window), :],
            (((1,), (1,)), ((), ())), preferred_element_type=f32)

    for n in range(count):
        here = pl.ds(n * rows, rows)
        two = long(bands[1], ibuf, n)
        y_ref[0, here, :] = (second[here, :].astype(f32) * two).astype(bf16)
        gs[1, here, :] = x_ref[3, here, :].astype(f32) * two
        gs[2, here, :] = long(adjs[0], hbuf, n)
        for k, (grad, src) in enumerate(((hbuf, vbuf), (gbuf, ibuf))):
            term = scores(grad, src, n)
            conv[k] = term if n == 0 else conv[k] + term

    for k in range(2):
        for h in range(2):
            turned = pltpu.roll(conv[k, pl.ds(h * rows, rows), :], 0, 1, stride=1, stride_axis=0)
            gfilt_ref[pl.ds(2 * k + h, 1), :] = jnp.sum(turned, axis=0, keepdims=True) / jnp.sqrt(
                jnp.float32(tokens * head_size))

    for c in range(3):
        sums = [jnp.zeros((8, chans), f32) for _ in range(3)]
        for n in range(count):
            here = pl.ds(n * rows, rows)
            g = gs[c, here, :]
            if n == count - 1:
                tail = jnp.zeros((8, chans), f32)
            else:
                tail = gs[c, pl.ds((n + 1) * rows, 8), :]
            wide = jnp.concatenate([g, tail], axis=0)
            y_ref[1 + c, here, :] = (
                sk_ref[c, 0:1] * g + sk_ref[c, 1:2] * wide[1:1 + rows] + sk_ref[c, 2:3] * wide[2:2 + rows]
            ).astype(bf16)
            for j, x in enumerate(delayed(c, n)):
                sums[j] = sums[j] + jnp.sum((g * x).reshape(rows // 8, 8, chans), axis=0)
        for j in range(3):
            gshort_ref[c, pl.ds(j, 1), :] = jnp.sum(sums[j], axis=0, keepdims=True) / jnp.sqrt(
                jnp.float32(tokens))


def by_channels(streams, short_kernel, filters, cotangent):
    f32, bf16 = jnp.float32, jnp.bfloat16
    rows = streams.shape[1]
    size = lax.axis_size("seq")
    me = lax.axis_index("seq")
    filt_len = filters.shape[2]
    tokens, chans = rows * size, streams.shape[2] // size
    window = filt_len + rows
    x = jnp.concatenate([streams, cotangent[None]], axis=0)
    x = lax.all_to_all(x, "seq", split_axis=2, concat_axis=1, tiled=True)
    sk = lax.dynamic_slice_in_dim(short_kernel, me * chans, chans, 2)
    taps = lax.dynamic_slice_in_dim(filters.astype(bf16).astype(f32), me * 2, 2, 1).reshape(4, filt_len)
    fwd = jnp.pad(taps[:, ::-1], ((0, 0), (1, rows - 1)))
    adj = jnp.pad(taps, ((0, 0), (0, rows)))
    y, gshort, gfilt = pl.pallas_call(
        functools.partial(local_kernel, rows, filt_len),
        out_shape=(
            jax.ShapeDtypeStruct((4, tokens, chans), bf16),
            jax.ShapeDtypeStruct((3, 3, chans), f32),
            jax.ShapeDtypeStruct((4, window), f32),
        ),
        scratch_shapes=[
            pltpu.VMEM((2, 2 * rows, window), bf16),
            pltpu.VMEM((2, 2 * rows, window), bf16),
            pltpu.VMEM((tokens + filt_len, chans), bf16),
            pltpu.VMEM((tokens + filt_len, chans), bf16),
            pltpu.VMEM((tokens + filt_len, chans), bf16),
            pltpu.VMEM((tokens + filt_len, chans), bf16),
            pltpu.VMEM((tokens, chans), bf16),
            pltpu.VMEM((tokens, chans), bf16),
            pltpu.VMEM((2, 2 * rows, window), f32),
            pltpu.VMEM((3, tokens, chans), f32),
        ],
        compiler_params=pltpu.CompilerParams(vmem_limit_bytes=48 * 1024 * 1024),
    )(x, sk, fwd, adj)
    y = lax.all_to_all(y, "seq", split_axis=1, concat_axis=2, tiled=True)
    grad_short = lax.all_gather(gshort, "seq", axis=2, tiled=True)
    gfilt = gfilt[:, rows:][:, ::-1].reshape(2, 2, filt_len)
    grad_filters = lax.all_gather(gfilt, "seq", axis=1, tiled=True)
    return (y[0], y[1:], grad_short, grad_filters)


def on_any(streams, short_kernel, filters, cotangent):
    whole_pairs = streams.shape[2] == 128 * lax.axis_size("seq") and filters.shape[1] == 2 * lax.axis_size("seq")
    form = by_channels if whole_pairs else on_device
    return form(streams, short_kernel, filters, cotangent)


def solution(mesh):
    placed = (P(None, ("groups", "seq"), None), P(), P(), P(("groups", "seq"), None))
    return jax.shard_map(
        on_any,
        mesh=mesh,
        in_specs=placed,
        out_specs=(
            P(("groups", "seq"), None),
            P(None, ("groups", "seq"), None),
            P("groups", None, None),
            P("groups", None, None),
        ),
        check_vma=False,
    )
```

```python
import functools

import jax
import jax.numpy as jnp
from jax import lax
from jax.experimental import pallas as pl
from jax.experimental.pallas import tpu as pltpu
from jax.sharding import PartitionSpec as P

GROUP = 4
LANES = 128


def hyena_kernel(rows, filt_len, seq, group,
                 streams, cot, sk_ref, fwd_ref, adj_ref,
                 out_hbm, grads_hbm, gshort_ref, gfilt_ref,
                 x_ref, y_ref, rim, grim, bands, adjs, vbuf, ibuf, gbuf, hbuf, first, second, score, gs,
                 pshort, pfilt, fshort, ffilt,
                 own_sem, in_send, in_recv, back_send, back_recv, out_own,
                 rim_send, rim_recv, halo_send, halo_recv, part_send, part_recv, full_send, full_recv):
    f32, bf16 = jnp.float32, jnp.bfloat16
    tokens, chans = x_ref.shape[1], x_ref.shape[2]
    count = tokens // rows
    window = filt_len + rows
    pairs = chans // LANES
    heads = 2 * pairs
    half = LANES // 2
    far = seq // group
    me = lax.axis_index("seq")
    z = lax.div(me, group)
    w = lax.rem(me, group)
    mine = pl.ds(pl.multiple_of(w * rows, rows), rows)
    cols = pl.ds(pl.multiple_of(w * chans, chans), chans)
    partners = [lax.rem(w + o, group) for o in range(1, group)]
    others = [lax.rem(z + o, far) for o in range(1, far)]

    def near(k):
        return {"seq": z * group + k}

    def along(k):
        return {"seq": k * group + w}

    barrier = pltpu.get_barrier_semaphore()
    for k in partners:
        pl.semaphore_signal(barrier, inc=1, device_id=near(k), device_id_type=pl.DeviceIdType.MESH)
    for k in others:
        pl.semaphore_signal(barrier, inc=1, device_id=along(k), device_id_type=pl.DeviceIdType.MESH)
    pl.semaphore_wait(barrier, group - 1 + far - 1)

    def remote(src, dst, send, recv, device):
        return pltpu.make_async_remote_copy(
            src_ref=src, dst_ref=dst, send_sem=send, recv_sem=recv,
            device_id=device, device_id_type=pl.DeviceIdType.MESH)

    def chunk(c, where):
        return cot.at[:, where] if c == 3 else streams.at[c, :, where]

    entry, own = {}, {}
    for c in (2, 1, 3, 0):
        own[c] = pltpu.make_async_copy(chunk(c, cols), x_ref.at[c, mine, :], own_sem.at[c])
        own[c].start()
        for o, k in enumerate(partners):
            there = pl.ds(pl.multiple_of(k * chans, chans), chans)
            entry[c, o] = remote(chunk(c, there), x_ref.at[c, mine, :],
                                 in_send.at[c, o], in_recv.at[c, o], near(k))
            entry[c, o].start()

    def arrived(c):
        own[c].wait()
        for o in range(group - 1):
            entry[c, o].wait_recv()

    later = along(lax.rem(z + 1, far))
    sooner = along(lax.rem(z + far - 1, far))
    has_later = z < far - 1
    has_sooner = z > 0

    def to_later(copy):
        if far > 1:
            pl.when(has_later)(copy.start)

    def from_sooner(copy):
        if far > 1:
            pl.when(has_sooner)(copy.wait_recv)

    def to_sooner(copy):
        if far > 1:
            pl.when(has_sooner)(copy.start)

    def from_later(copy):
        if far > 1:
            pl.when(has_later)(copy.wait_recv)

    @pl.when(z == 0)
    def _():
        vbuf[pl.ds(0, filt_len), :] = jnp.zeros((filt_len, chans), bf16)
        ibuf[pl.ds(0, filt_len), :] = jnp.zeros((filt_len, chans), bf16)
        rim[...] = jnp.zeros(rim.shape, bf16)

    @pl.when(z == far - 1)
    def _():
        gbuf[pl.ds(tokens, filt_len), :] = jnp.zeros((filt_len, chans), bf16)
        hbuf[pl.ds(tokens, filt_len), :] = jnp.zeros((filt_len, chans), bf16)
        grim[...] = jnp.zeros(grim.shape, f32)

    for k in range(2):
        for h in range(heads):
            part = pl.ds((h % 2) * rows, rows)
            for src, dst in ((fwd_ref, bands), (adj_ref, adjs)):
                line = jnp.broadcast_to(src[pl.ds(k * heads + h, 1), :], (rows, window))
                dst[k, h // 2, part, :] = pltpu.roll(line, 0, 1, stride=1, stride_axis=0).astype(bf16)

    def delayed(c, n):
        x = x_ref[c, pl.ds(n * rows, rows), :].astype(f32)
        head = (rim[c] if n == 0 else x_ref[c, pl.ds(n * rows - 16, 16), :]).astype(f32)
        wide = jnp.concatenate([head, x], axis=0)
        return x, wide[15:15 + rows], wide[14:14 + rows]

    def short(c, n):
        x0, x1, x2 = delayed(c, n)
        return (sk_ref[c, 0:1] * x0 + sk_ref[c, 1:2] * x1 + sk_ref[c, 2:3] * x2).astype(bf16)

    rims = [remote(x_ref.at[c, pl.ds(tokens - 16, 16), :], rim.at[c], rim_send.at[c], rim_recv.at[c], later)
            for c in range(3)]
    tail, lead = pl.ds(tokens, filt_len), pl.ds(0, filt_len)
    halo_v = remote(vbuf.at[tail, :], vbuf.at[lead, :], halo_send.at[0], halo_recv.at[0], later)
    halo_g = remote(gbuf.at[lead, :], gbuf.at[tail, :], halo_send.at[1], halo_recv.at[1], sooner)
    halo_i = remote(ibuf.at[tail, :], ibuf.at[lead, :], halo_send.at[2], halo_recv.at[2], later)
    halo_h = remote(hbuf.at[lead, :], hbuf.at[tail, :], halo_send.at[3], halo_recv.at[3], sooner)

    def set_values(n):
        vbuf[pl.ds(filt_len + n * rows, rows), :] = short(2, n)

    arrived(2)
    to_later(rims[2])
    for n in range(1, count):
        set_values(n)
    if tokens == filt_len:
        from_sooner(rims[2])
        set_values(0)
    to_later(halo_v)
    arrived(1)
    to_later(rims[1])
    arrived(3)

    def set_second(n):
        here = pl.ds(n * rows, rows)
        gate = short(1, n)
        second[here, :] = gate
        gbuf[here, :] = (x_ref[3, here, :].astype(f32) * gate.astype(f32)).astype(bf16)

    for n in range(1, count):
        set_second(n)
    from_sooner(rims[1])
    set_second(0)
    to_sooner(halo_g)
    if tokens != filt_len:
        from_sooner(rims[2])
        set_values(0)
    arrived(0)
    to_later(rims[0])
    for n in range(1, count):
        first[pl.ds(n * rows, rows), :] = short(0, n)
    from_sooner(rims[0])
    first[pl.ds(0, rows), :] = short(0, 0)

    lane = lax.broadcasted_iota(jnp.int32, (rows, LANES), 1)

    def long(mats, k, src, n):
        parts = []
        for p in range(pairs):
            stacked = jnp.dot(mats[k, p], src[pl.ds(n * rows, window), p * LANES:(p + 1) * LANES],
                              preferred_element_type=f32)
            parts.append(jnp.where(lane < half, stacked[:rows], stacked[rows:]))
        return jnp.concatenate(parts, axis=1)

    from_sooner(halo_v)
    from_later(halo_g)
    for n in range(count):
        here = pl.ds(n * rows, rows)
        gate = first[here, :].astype(f32)
        one = long(bands, 0, vbuf, n)
        ibuf[pl.ds(filt_len + n * rows, rows), :] = (gate * one).astype(bf16)
        back = long(adjs, 1, gbuf, n)
        gs[0, here, :] = back * one
        hbuf[here, :] = (back * gate).astype(bf16)
    to_later(halo_i)
    to_sooner(halo_h)

    flip_r = lax.broadcasted_iota(jnp.int32, (rows, rows), 0)
    flip_c = lax.broadcasted_iota(jnp.int32, (rows, rows), 1)
    flip = (flip_r + flip_c == rows - 1).astype(f32).astype(bf16)

    def scores(k, grad, src):
        for p in range(pairs):
            total = None
            for n in range(count):
                span = slice(p * LANES, (p + 1) * LANES)
                turned = jnp.dot(flip, grad[pl.ds(n * rows, rows), span], preferred_element_type=f32)
                low = jnp.where(lane < half, turned, 0.0).astype(bf16)
                high = jnp.where(lane < half, 0.0, turned).astype(bf16)
                term = lax.dot_general(
                    jnp.concatenate([low, high], axis=0), src[pl.ds(n * rows, window), span],
                    (((1,), (1,)), ((), ())), preferred_element_type=f32)
                total = term if total is None else total + term
            score[...] = total
            for h in range(2):
                turned = pltpu.roll(score[pl.ds(h * rows, rows), :], 0, 1, stride=1, stride_axis=0)
                pfilt[z, pl.ds(k * heads + 2 * p + h, 1), :] = jnp.sum(turned, axis=0, keepdims=True)

    scores(0, hbuf, vbuf)
    from_sooner(halo_i)
    for n in range(count):
        here = pl.ds(n * rows, rows)
        two = long(bands, 1, ibuf, n)
        y_ref[0, here, :] = (second[here, :].astype(f32) * two).astype(bf16)
        gs[1, here, :] = x_ref[3, here, :].astype(f32) * two

    def back_copy(c, o, k):
        dst = out_hbm.at[:, cols] if c == 0 else grads_hbm.at[c - 1, :, cols]
        rows_k = pl.ds(pl.multiple_of(k * rows, rows), rows)
        return remote(y_ref.at[c, rows_k, :], dst, back_send.at[c, o], back_recv.at[c, o], near(k))

    home, exits = {}, {}

    def send_back(c):
        for o, k in enumerate(partners):
            exits[c, o] = back_copy(c, o, k)
            exits[c, o].start()
        dst = out_hbm.at[:, cols] if c == 0 else grads_hbm.at[c - 1, :, cols]
        home[c] = pltpu.make_async_copy(y_ref.at[c, mine, :], dst, out_own.at[c])
        home[c].start()

    grims = [remote(gs.at[c, pl.ds(0, 8), :], grim.at[c], rim_send.at[3 + c], rim_recv.at[3 + c], sooner)
             for c in range(3)]
    to_sooner(grims[0])
    to_sooner(grims[1])
    send_back(0)

    def stream_grads(c):
        from_later(grims[c])
        for n in range(count):
            here = pl.ds(n * rows, rows)
            g = gs[c, here, :]
            after = grim[c] if n == count - 1 else gs[c, pl.ds((n + 1) * rows, 8), :]
            wide = jnp.concatenate([g, after], axis=0)
            y_ref[1 + c, here, :] = (
                sk_ref[c, 0:1] * g + sk_ref[c, 1:2] * wide[1:1 + rows] + sk_ref[c, 2:3] * wide[2:2 + rows]
            ).astype(bf16)
        send_back(1 + c)

    stream_grads(0)
    from_later(halo_h)
    for n in range(count):
        gs[2, pl.ds(n * rows, rows), :] = long(adjs, 0, hbuf, n)
    to_sooner(grims[2])
    stream_grads(1)
    stream_grads(2)
    scores(1, gbuf, ibuf)
    for c in range(3):
        sums = [jnp.zeros((8, chans), f32) for _ in range(3)]
        for n in range(count):
            g = gs[c, pl.ds(n * rows, rows), :]
            for j, x in enumerate(delayed(c, n)):
                sums[j] = sums[j] + jnp.sum((g * x).reshape(rows // 8, 8, chans), axis=0)
        for j in range(3):
            pshort[z, pl.ds(3 * c + j, 1), :] = jnp.sum(sums[j], axis=0, keepdims=True)
    pshort[z, pl.ds(9, 7), :] = jnp.zeros((7, chans), f32)

    parts = []
    for o, k in enumerate(others):
        for i, ref in enumerate((pshort, pfilt)):
            copy = remote(ref.at[z], ref.at[z], part_send.at[i, o], part_recv.at[i, o], along(k))
            copy.start()
            parts.append(copy)
    for copy in parts:
        copy.wait_recv()
    total = float(rows * seq)
    fshort[w] = jnp.sum(pshort[...], axis=0) / jnp.sqrt(jnp.float32(total))
    ffilt[w] = jnp.sum(pfilt[...], axis=0) / jnp.sqrt(jnp.float32(total * half))
    fulls = []
    for o, k in enumerate(partners):
        for i, ref in enumerate((fshort, ffilt)):
            copy = remote(ref.at[w], ref.at[w], full_send.at[i, o], full_recv.at[i, o], near(k))
            copy.start()
            fulls.append(copy)
    for copy in fulls:
        copy.wait_recv()
    gshort_ref[...] = fshort[...]
    gfilt_ref[...] = ffilt[...]
    for copy in home.values():
        copy.wait()
    for copy in exits.values():
        copy.wait_recv()
    for copy in list(entry.values()) + list(exits.values()) + parts + fulls:
        copy.wait_send()
    if far > 1:
        for copy in rims + [halo_v, halo_i]:
            pl.when(has_later)(copy.wait_send)
        for copy in grims + [halo_g, halo_h]:
            pl.when(has_sooner)(copy.wait_send)


def on_device(streams, short_kernel, filters, cotangent):
    f32, bf16 = jnp.float32, jnp.bfloat16
    rows, width = streams.shape[1], streams.shape[2]
    seq = lax.axis_size("seq")
    filt_len = filters.shape[2]
    group = GROUP
    far = seq // group
    w = lax.rem(lax.axis_index("seq"), group)
    tokens, chans = rows * group, width // group
    heads = filters.shape[1] // group
    pairs = chans // LANES
    window = filt_len + rows
    sk = lax.dynamic_slice_in_dim(short_kernel, w * chans, chans, 2)
    taps = lax.dynamic_slice_in_dim(filters, w * heads, heads, 1).astype(bf16).astype(f32).reshape(2 * heads, filt_len)
    fwd = jnp.pad(taps[:, ::-1], ((0, 0), (1, rows - 1)))
    adj = jnp.pad(taps, ((0, 0), (0, rows)))
    hbm = pl.BlockSpec(memory_space=pl.ANY)
    vmem = pl.BlockSpec(memory_space=pltpu.VMEM)
    dma = pltpu.SemaphoreType.DMA
    output, grad_streams, gshort, gfilt = pl.pallas_call(
        functools.partial(hyena_kernel, rows, filt_len, seq, group),
        out_shape=(
            jax.ShapeDtypeStruct((rows, width), bf16),
            jax.ShapeDtypeStruct((3, rows, width), bf16),
            jax.ShapeDtypeStruct((group, 16, chans), f32),
            jax.ShapeDtypeStruct((group, 2 * heads, window), f32),
        ),
        in_specs=[hbm, hbm, vmem, vmem, vmem],
        out_specs=(hbm, hbm, vmem, vmem),
        scratch_shapes=[
            pltpu.VMEM((4, tokens, chans), bf16),
            pltpu.VMEM((4, tokens, chans), bf16),
            pltpu.VMEM((3, 16, chans), bf16),
            pltpu.VMEM((3, 8, chans), f32),
            pltpu.VMEM((2, pairs, 2 * rows, window), bf16),
            pltpu.VMEM((2, pairs, 2 * rows, window), bf16),
            pltpu.VMEM((tokens + filt_len, chans), bf16),
            pltpu.VMEM((tokens + filt_len, chans), bf16),
            pltpu.VMEM((tokens + filt_len, chans), bf16),
            pltpu.VMEM((tokens + filt_len, chans), bf16),
            pltpu.VMEM((tokens, chans), bf16),
            pltpu.VMEM((tokens, chans), bf16),
            pltpu.VMEM((2 * rows, window), f32),
            pltpu.VMEM((3, tokens, chans), f32),
            pltpu.VMEM((far, 16, chans), f32),
            pltpu.VMEM((far, 2 * heads, window), f32),
            pltpu.VMEM((group, 16, chans), f32),
            pltpu.VMEM((group, 2 * heads, window), f32),
            dma((4,)),
            dma((4, group - 1)),
            dma((4, group - 1)),
            dma((4, group - 1)),
            dma((4, group - 1)),
            dma((4,)),
            dma((6,)),
            dma((6,)),
            dma((4,)),
            dma((4,)),
            dma((2, max(far - 1, 1))),
            dma((2, max(far - 1, 1))),
            dma((2, group - 1)),
            dma((2, group - 1)),
        ],
        compiler_params=pltpu.CompilerParams(
            vmem_limit_bytes=48 * 1024 * 1024, collective_id=0, has_side_effects=True),
    )(streams, cotangent, sk, fwd, adj)
    grad_short = gshort[:, :9].reshape(group, 3, 3, chans).transpose(1, 2, 0, 3).reshape(3, 3, width)
    gfilt = gfilt[:, :, rows:][:, :, ::-1].reshape(group, 2, heads, filt_len)
    grad_filters = gfilt.transpose(1, 0, 2, 3).reshape(2, group * heads, filt_len)
    return (output, grad_streams, grad_short, grad_filters)


def solution(mesh):
    placed = (P(None, ("groups", "seq"), None), P(), P(), P(("groups", "seq"), None))
    return jax.shard_map(
        on_device,
        mesh=mesh,
        in_specs=placed,
        out_specs=(
            P(("groups", "seq"), None),
            P(None, ("groups", "seq"), None),
            P("groups", None, None),
            P("groups", None, None),
        ),
        check_vma=False,
    )
```

```python
import functools

import jax
import jax.numpy as jnp
from jax import lax
from jax.experimental import pallas as pl
from jax.experimental.pallas import tpu as pltpu
from jax.sharding import PartitionSpec as P

GROUP = 4
AHEAD = 2
LANES = 128


def hyena_kernel(rows, filt_len, seq, group,
                 streams, cot, sk_ref, fwd_ref, adj_ref,
                 out_hbm, grads_hbm, gshort_ref, gfilt_ref,
                 x_ref, y_ref, rim, grim, bands, adjs, vbuf, ibuf, gbuf, hbuf, first, second, score, gs,
                 pshort, pfilt, fshort, ffilt,
                 own_sem, in_send, in_recv, back_send, back_recv, out_own,
                 rim_send, rim_recv, halo_send, halo_recv, part_send, part_recv, full_send, full_recv):
    f32, bf16 = jnp.float32, jnp.bfloat16
    tokens, chans = x_ref.shape[1], x_ref.shape[2]
    count = tokens // rows
    window = filt_len + rows
    pairs = chans // LANES
    heads = 2 * pairs
    half = LANES // 2
    far = seq // group
    me = lax.axis_index("seq")
    z = lax.div(me, group)
    w = lax.rem(me, group)
    mine = pl.ds(pl.multiple_of(w * rows, rows), rows)
    partners = [lax.rem(w + o, group) for o in range(1, group)]
    others = [lax.rem(z + o, far) for o in range(1, far)]

    def near(k):
        return {"seq": z * group + k}

    def along(k):
        return {"seq": k * group + w}

    barrier = pltpu.get_barrier_semaphore()
    for k in partners:
        pl.semaphore_signal(barrier, inc=1, device_id=near(k), device_id_type=pl.DeviceIdType.MESH)
    for k in others:
        pl.semaphore_signal(barrier, inc=1, device_id=along(k), device_id_type=pl.DeviceIdType.MESH)
    pl.semaphore_wait(barrier, group - 1 + far - 1)

    def remote(src, dst, send, recv, device):
        return pltpu.make_async_remote_copy(
            src_ref=src, dst_ref=dst, send_sem=send, recv_sem=recv,
            device_id=device, device_id_type=pl.DeviceIdType.MESH)

    def span(q):
        return slice(q * LANES, (q + 1) * LANES)

    def lanes_of(k, q):
        return pl.ds(pl.multiple_of(k * chans + q * LANES, LANES), LANES)

    def source(i, where):
        return cot.at[:, where] if i else streams.at[:, :, where]

    def landing(i, q):
        return x_ref.at[3, mine, span(q)] if i else x_ref.at[pl.ds(0, 3), mine, span(q)]

    entry, own = {}, {}

    def enter(q):
        for i in range(2):
            for o, k in enumerate(partners):
                entry[q, i, o] = remote(source(i, lanes_of(k, q)), landing(i, q),
                                        in_send.at[2 * q + i, o], in_recv.at[2 * q + i, o], near(k))
                entry[q, i, o].start()
            own[q, i] = pltpu.make_async_copy(source(i, lanes_of(w, q)), landing(i, q), own_sem.at[2 * q + i])
            own[q, i].start()

    def arrived(q):
        for i in range(2):
            own[q, i].wait()
            for o in range(group - 1):
                entry[q, i, o].wait_recv()

    for q in range(min(AHEAD, pairs)):
        enter(q)

    later = along(lax.rem(z + 1, far))
    sooner = along(lax.rem(z + far - 1, far))
    has_later = z < far - 1
    has_sooner = z > 0

    def to_later(copy):
        if far > 1:
            pl.when(has_later)(copy.start)

    def from_sooner(copy):
        if far > 1:
            pl.when(has_sooner)(copy.wait_recv)

    def to_sooner(copy):
        if far > 1:
            pl.when(has_sooner)(copy.start)

    def from_later(copy):
        if far > 1:
            pl.when(has_later)(copy.wait_recv)

    @pl.when(z == 0)
    def _():
        vbuf[pl.ds(0, filt_len), :] = jnp.zeros((filt_len, chans), bf16)
        ibuf[pl.ds(0, filt_len), :] = jnp.zeros((filt_len, chans), bf16)
        rim[...] = jnp.zeros(rim.shape, bf16)

    @pl.when(z == far - 1)
    def _():
        gbuf[pl.ds(tokens, filt_len), :] = jnp.zeros((filt_len, chans), bf16)
        hbuf[pl.ds(tokens, filt_len), :] = jnp.zeros((filt_len, chans), bf16)
        grim[...] = jnp.zeros(grim.shape, f32)

    for k in range(2):
        for h in range(heads):
            part = pl.ds((h % 2) * rows, rows)
            for src, dst in ((fwd_ref, bands), (adj_ref, adjs)):
                line = jnp.broadcast_to(src[pl.ds(k * heads + h, 1), :], (rows, window))
                dst[k, h // 2, part, :] = pltpu.roll(line, 0, 1, stride=1, stride_axis=0).astype(bf16)

    def delayed(c, n, q):
        x = x_ref[c, pl.ds(n * rows, rows), span(q)].astype(f32)
        head = (rim[c, :, span(q)] if n == 0 else x_ref[c, pl.ds(n * rows - 16, 16), span(q)]).astype(f32)
        wide = jnp.concatenate([head, x], axis=0)
        return x, wide[15:15 + rows], wide[14:14 + rows]

    def tap(c, j, q):
        return sk_ref[c, j:j + 1, span(q)]

    def short(c, n, q):
        x0, x1, x2 = delayed(c, n, q)
        return (tap(c, 0, q) * x0 + tap(c, 1, q) * x1 + tap(c, 2, q) * x2).astype(bf16)

    tail, lead = pl.ds(tokens, filt_len), pl.ds(0, filt_len)
    rims, grims, halos_later, halos_sooner = [], [], {}, {}
    for q in range(pairs):
        rims.append(remote(x_ref.at[pl.ds(0, 3), pl.ds(tokens - 16, 16), span(q)], rim.at[:, :, span(q)],
                           rim_send.at[q], rim_recv.at[q], later))
        grims.append(remote(gs.at[:, pl.ds(0, 8), span(q)], grim.at[:, :, span(q)],
                            rim_send.at[pairs + q], rim_recv.at[pairs + q], sooner))
        for i, ref in enumerate((vbuf, ibuf)):
            halos_later[q, i] = remote(ref.at[tail, span(q)], ref.at[lead, span(q)],
                                       halo_send.at[4 * q + i], halo_recv.at[4 * q + i], later)
        for i, ref in enumerate((gbuf, hbuf)):
            halos_sooner[q, i] = remote(ref.at[lead, span(q)], ref.at[tail, span(q)],
                                        halo_send.at[4 * q + 2 + i], halo_recv.at[4 * q + 2 + i], sooner)

    lane = lax.broadcasted_iota(jnp.int32, (rows, LANES), 1)

    def long(mats, k, src, n, q):
        stacked = jnp.dot(mats[k, q], src[pl.ds(n * rows, window), span(q)], preferred_element_type=f32)
        return jnp.where(lane < half, stacked[:rows], stacked[rows:])

    flip_r = lax.broadcasted_iota(jnp.int32, (rows, rows), 0)
    flip_c = lax.broadcasted_iota(jnp.int32, (rows, rows), 1)
    flip = (flip_r + flip_c == rows - 1).astype(f32).astype(bf16)

    def scores(k, grad, src, q):
        total = None
        for n in range(count):
            turned = jnp.dot(flip, grad[pl.ds(n * rows, rows), span(q)], preferred_element_type=f32)
            low = jnp.where(lane < half, turned, 0.0).astype(bf16)
            high = jnp.where(lane < half, 0.0, turned).astype(bf16)
            term = lax.dot_general(
                jnp.concatenate([low, high], axis=0), src[pl.ds(n * rows, window), span(q)],
                (((1,), (1,)), ((), ())), preferred_element_type=f32)
            total = term if total is None else total + term
        score[...] = total
        for h in range(2):
            turned = pltpu.roll(score[pl.ds(h * rows, rows), :], 0, 1, stride=1, stride_axis=0)
            pfilt[z, pl.ds(k * heads + 2 * q + h, 1), :] = jnp.sum(turned, axis=0, keepdims=True)

    home, exits = {}, {}

    def send_back(i, q):
        def piece(k):
            there = pl.ds(pl.multiple_of(k * rows, rows), rows)
            return y_ref.at[pl.ds(1, 3), there, span(q)] if i else y_ref.at[0, there, span(q)]

        dst = grads_hbm.at[:, :, lanes_of(w, q)] if i else out_hbm.at[:, lanes_of(w, q)]
        for o, k in enumerate(partners):
            exits[q, i, o] = remote(piece(k), dst, back_send.at[2 * q + i, o], back_recv.at[2 * q + i, o], near(k))
            exits[q, i, o].start()
        home[q, i] = pltpu.make_async_copy(piece(w), dst, out_own.at[2 * q + i])
        home[q, i].start()

    def stage_enter(q):
        arrived(q)
        if q + AHEAD < pairs:
            enter(q + AHEAD)
        to_later(rims[q])

    def stage_short(q):
        from_sooner(rims[q])
        for n in range(count):
            vbuf[pl.ds(filt_len + n * rows, rows), span(q)] = short(2, n, q)
        to_later(halos_later[q, 0])
        for n in range(count):
            here = pl.ds(n * rows, rows)
            gate = short(1, n, q)
            second[here, span(q)] = gate
            gbuf[here, span(q)] = (x_ref[3, here, span(q)].astype(f32) * gate.astype(f32)).astype(bf16)
        to_sooner(halos_sooner[q, 0])
        for n in range(count):
            first[pl.ds(n * rows, rows), span(q)] = short(0, n, q)

    def stage_inner(q):
        from_sooner(halos_later[q, 0])
        from_later(halos_sooner[q, 0])
        for n in range(count):
            here = pl.ds(n * rows, rows)
            gate = first[here, span(q)].astype(f32)
            one = long(bands, 0, vbuf, n, q)
            ibuf[pl.ds(filt_len + n * rows, rows), span(q)] = (gate * one).astype(bf16)
            back = long(adjs, 1, gbuf, n, q)
            gs[0, here, span(q)] = back * one
            hbuf[here, span(q)] = (back * gate).astype(bf16)
        to_later(halos_later[q, 1])
        to_sooner(halos_sooner[q, 1])

    def stage_outer(q):
        from_sooner(halos_later[q, 1])
        from_later(halos_sooner[q, 1])
        for n in range(count):
            here = pl.ds(n * rows, rows)
            two = long(bands, 1, ibuf, n, q)
            y_ref[0, here, span(q)] = (second[here, span(q)].astype(f32) * two).astype(bf16)
            gs[1, here, span(q)] = x_ref[3, here, span(q)].astype(f32) * two
            gs[2, here, span(q)] = long(adjs, 0, hbuf, n, q)
        to_sooner(grims[q])
        send_back(0, q)

    def stage_grads(q):
        from_later(grims[q])
        for c in range(3):
            for n in range(count):
                here = pl.ds(n * rows, rows)
                g = gs[c, here, span(q)]
                after = grim[c, :, span(q)] if n == count - 1 else gs[c, pl.ds((n + 1) * rows, 8), span(q)]
                wide = jnp.concatenate([g, after], axis=0)
                y_ref[1 + c, here, span(q)] = (
                    tap(c, 0, q) * g + tap(c, 1, q) * wide[1:1 + rows] + tap(c, 2, q) * wide[2:2 + rows]
                ).astype(bf16)
        send_back(1, q)

    def stage_sums(q):
        scores(0, hbuf, vbuf, q)
        scores(1, gbuf, ibuf, q)
        for c in range(3):
            sums = [jnp.zeros((8, LANES), f32) for _ in range(3)]
            for n in range(count):
                g = gs[c, pl.ds(n * rows, rows), span(q)]
                for j, x in enumerate(delayed(c, n, q)):
                    sums[j] = sums[j] + jnp.sum((g * x).reshape(rows // 8, 8, LANES), axis=0)
            for j in range(3):
                pshort[z, pl.ds(3 * c + j, 1), span(q)] = jnp.sum(sums[j], axis=0, keepdims=True)

    pshort[z, pl.ds(9, 7), :] = jnp.zeros((7, chans), f32)
    for t in range(pairs + 3):
        for stage, q in ((stage_inner, t - 1), (stage_grads, t - 2), (stage_enter, t),
                         (stage_outer, t - 1), (stage_short, t), (stage_sums, t - 3)):
            if 0 <= q < pairs:
                stage(q)

    parts = []
    for o, k in enumerate(others):
        for i, ref in enumerate((pshort, pfilt)):
            copy = remote(ref.at[z], ref.at[z], part_send.at[i, o], part_recv.at[i, o], along(k))
            copy.start()
            parts.append(copy)
    for copy in parts:
        copy.wait_recv()
    total = float(rows * seq)
    fshort[w] = jnp.sum(pshort[...], axis=0) / jnp.sqrt(jnp.float32(total))
    ffilt[w] = jnp.sum(pfilt[...], axis=0) / jnp.sqrt(jnp.float32(total * half))
    fulls = []
    for o, k in enumerate(partners):
        for i, ref in enumerate((fshort, ffilt)):
            copy = remote(ref.at[w], ref.at[w], full_send.at[i, o], full_recv.at[i, o], near(k))
            copy.start()
            fulls.append(copy)
    for copy in fulls:
        copy.wait_recv()
    gshort_ref[...] = fshort[...]
    gfilt_ref[...] = ffilt[...]
    for copy in home.values():
        copy.wait()
    for copy in exits.values():
        copy.wait_recv()
    for copy in list(entry.values()) + list(exits.values()) + parts + fulls:
        copy.wait_send()
    if far > 1:
        for copy in rims + list(halos_later.values()):
            pl.when(has_later)(copy.wait_send)
        for copy in grims + list(halos_sooner.values()):
            pl.when(has_sooner)(copy.wait_send)


def on_device(streams, short_kernel, filters, cotangent):
    f32, bf16 = jnp.float32, jnp.bfloat16
    rows, width = streams.shape[1], streams.shape[2]
    seq = lax.axis_size("seq")
    filt_len = filters.shape[2]
    group = GROUP
    far = seq // group
    w = lax.rem(lax.axis_index("seq"), group)
    tokens, chans = rows * group, width // group
    heads = filters.shape[1] // group
    pairs = chans // LANES
    window = filt_len + rows
    sk = lax.dynamic_slice_in_dim(short_kernel, w * chans, chans, 2)
    taps = lax.dynamic_slice_in_dim(filters, w * heads, heads, 1).astype(bf16).astype(f32).reshape(2 * heads, filt_len)
    fwd = jnp.pad(taps[:, ::-1], ((0, 0), (1, rows - 1)))
    adj = jnp.pad(taps, ((0, 0), (0, rows)))
    hbm = pl.BlockSpec(memory_space=pltpu.HBM)
    vmem = pl.BlockSpec(memory_space=pltpu.VMEM)
    dma = pltpu.SemaphoreType.DMA
    output, grad_streams, gshort, gfilt = pl.pallas_call(
        functools.partial(hyena_kernel, rows, filt_len, seq, group),
        out_shape=(
            jax.ShapeDtypeStruct((rows, width), bf16),
            jax.ShapeDtypeStruct((3, rows, width), bf16),
            jax.ShapeDtypeStruct((group, 16, chans), f32),
            jax.ShapeDtypeStruct((group, 2 * heads, window), f32),
        ),
        in_specs=[hbm, hbm, vmem, vmem, vmem],
        out_specs=(hbm, hbm, vmem, vmem),
        scratch_shapes=[
            pltpu.VMEM((4, tokens, chans), bf16),
            pltpu.VMEM((4, tokens, chans), bf16),
            pltpu.VMEM((3, 16, chans), bf16),
            pltpu.VMEM((3, 8, chans), f32),
            pltpu.VMEM((2, pairs, 2 * rows, window), bf16),
            pltpu.VMEM((2, pairs, 2 * rows, window), bf16),
            pltpu.VMEM((tokens + filt_len, chans), bf16),
            pltpu.VMEM((tokens + filt_len, chans), bf16),
            pltpu.VMEM((tokens + filt_len, chans), bf16),
            pltpu.VMEM((tokens + filt_len, chans), bf16),
            pltpu.VMEM((tokens, chans), bf16),
            pltpu.VMEM((tokens, chans), bf16),
            pltpu.VMEM((2 * rows, window), f32),
            pltpu.VMEM((3, tokens, chans), f32),
            pltpu.VMEM((far, 16, chans), f32),
            pltpu.VMEM((far, 2 * heads, window), f32),
            pltpu.VMEM((group, 16, chans), f32),
            pltpu.VMEM((group, 2 * heads, window), f32),
            dma((2 * pairs,)),
            dma((2 * pairs, group - 1)),
            dma((2 * pairs, group - 1)),
            dma((2 * pairs, group - 1)),
            dma((2 * pairs, group - 1)),
            dma((2 * pairs,)),
            dma((2 * pairs,)),
            dma((2 * pairs,)),
            dma((4 * pairs,)),
            dma((4 * pairs,)),
            dma((2, max(far - 1, 1))),
            dma((2, max(far - 1, 1))),
            dma((2, group - 1)),
            dma((2, group - 1)),
        ],
        compiler_params=pltpu.CompilerParams(
            vmem_limit_bytes=62 * 1024 * 1024, collective_id=0, has_side_effects=True),
    )(streams, cotangent, sk, fwd, adj)
    grad_short = gshort[:, :9].reshape(group, 3, 3, chans).transpose(1, 2, 0, 3).reshape(3, 3, width)
    gfilt = gfilt[:, :, rows:][:, :, ::-1].reshape(group, 2, heads, filt_len)
    grad_filters = gfilt.transpose(1, 0, 2, 3).reshape(2, group * heads, filt_len)
    return (output, grad_streams, grad_short, grad_filters)


def solution(mesh):
    placed = (P(None, ("groups", "seq"), None), P(), P(), P(("groups", "seq"), None))
    return jax.shard_map(
        on_device,
        mesh=mesh,
        in_specs=placed,
        out_specs=(
            P(("groups", "seq"), None),
            P(None, ("groups", "seq"), None),
            P("groups", None, None),
            P("groups", None, None),
        ),
        check_vma=False,
    )
```

```python
import functools

import jax
import jax.numpy as jnp
from jax import lax
from jax.experimental import pallas as pl
from jax.experimental.pallas import tpu as pltpu
from jax.sharding import PartitionSpec as P

GROUP = 4
AHEAD = 4
WIDTH = 128
LANES = 128


def hyena_kernel(rows, filt_len, seq, group,
                 streams, cot, sk_ref, fwd_ref, adj_ref,
                 out_hbm, grads_hbm, gshort_ref, gfilt_ref,
                 x_ref, y_ref, rim, grim, bands, adjs, vbuf, ibuf, gbuf, hbuf, first, second, score, gs,
                 pshort, pfilt, fshort, ffilt,
                 own_sem, in_send, in_recv, back_send, back_recv, out_own,
                 rim_send, rim_recv, halo_send, halo_recv, part_send, part_recv, full_send, full_recv):
    f32, bf16 = jnp.float32, jnp.bfloat16
    tokens, chans = x_ref.shape[1], x_ref.shape[2]
    count = tokens // rows
    window = filt_len + rows
    pairs = chans // LANES
    heads = 2 * pairs
    slabs = chans // WIDTH
    half = LANES // 2
    far = seq // group
    me = lax.axis_index("seq")
    z = lax.div(me, group)
    w = lax.rem(me, group)
    mine = pl.ds(pl.multiple_of(w * rows, rows), rows)
    partners = [lax.rem(w + o, group) for o in range(1, group)]
    others = [lax.rem(z + o, far) for o in range(1, far)]

    def near(k):
        return {"seq": z * group + k}

    def along(k):
        return {"seq": k * group + w}

    barrier = pltpu.get_barrier_semaphore()
    for k in partners:
        pl.semaphore_signal(barrier, inc=1, device_id=near(k), device_id_type=pl.DeviceIdType.MESH)
    for k in others:
        pl.semaphore_signal(barrier, inc=1, device_id=along(k), device_id_type=pl.DeviceIdType.MESH)
    pl.semaphore_wait(barrier, group - 1 + far - 1)

    def remote(src, dst, send, recv, device):
        return pltpu.make_async_remote_copy(
            src_ref=src, dst_ref=dst, send_sem=send, recv_sem=recv,
            device_id=device, device_id_type=pl.DeviceIdType.MESH)

    def span(q):
        return slice(q * WIDTH, (q + 1) * WIDTH)

    def lanes_of(k, q):
        return pl.ds(pl.multiple_of(k * chans + q * WIDTH, WIDTH), WIDTH)

    def source(i, where):
        return cot.at[:, where] if i else streams.at[:, :, where]

    def landing(i, q):
        return x_ref.at[3, mine, span(q)] if i else x_ref.at[pl.ds(0, 3), mine, span(q)]

    entry, own = {}, {}

    def enter(q):
        for i in range(2):
            for o, k in enumerate(partners):
                entry[q, i, o] = remote(source(i, lanes_of(k, q)), landing(i, q),
                                        in_send.at[2 * q + i, o], in_recv.at[2 * q + i, o], near(k))
                entry[q, i, o].start()
            own[q, i] = pltpu.make_async_copy(source(i, lanes_of(w, q)), landing(i, q), own_sem.at[2 * q + i])
            own[q, i].start()

    def arrived(q):
        for i in range(2):
            own[q, i].wait()
            for o in range(group - 1):
                entry[q, i, o].wait_recv()

    for q in range(min(AHEAD, slabs)):
        enter(q)

    later = along(lax.rem(z + 1, far))
    sooner = along(lax.rem(z + far - 1, far))
    has_later = z < far - 1
    has_sooner = z > 0

    def to_later(copy):
        if far > 1:
            pl.when(has_later)(copy.start)

    def from_sooner(copy):
        if far > 1:
            pl.when(has_sooner)(copy.wait_recv)

    def to_sooner(copy):
        if far > 1:
            pl.when(has_sooner)(copy.start)

    def from_later(copy):
        if far > 1:
            pl.when(has_later)(copy.wait_recv)

    @pl.when(z == 0)
    def _():
        vbuf[pl.ds(0, filt_len), :] = jnp.zeros((filt_len, chans), bf16)
        ibuf[pl.ds(0, filt_len), :] = jnp.zeros((filt_len, chans), bf16)
        rim[...] = jnp.zeros(rim.shape, bf16)

    @pl.when(z == far - 1)
    def _():
        gbuf[pl.ds(tokens, filt_len), :] = jnp.zeros((filt_len, chans), bf16)
        hbuf[pl.ds(tokens, filt_len), :] = jnp.zeros((filt_len, chans), bf16)
        grim[...] = jnp.zeros(grim.shape, f32)

    def make_bands(q):
        for k in range(2):
            for h in range(2 * q * WIDTH // LANES, 2 * (q + 1) * WIDTH // LANES):
                part = pl.ds((h % 2) * rows, rows)
                for src, dst in ((fwd_ref, bands), (adj_ref, adjs)):
                    line = jnp.broadcast_to(src[pl.ds(k * heads + h, 1), :], (rows, window))
                    dst[k, h // 2, part, :] = pltpu.roll(line, 0, 1, stride=1, stride_axis=0).astype(bf16)

    def delayed(c, n, q):
        x = x_ref[c, pl.ds(n * rows, rows), span(q)].astype(f32)
        head = (rim[c, :, span(q)] if n == 0 else x_ref[c, pl.ds(n * rows - 16, 16), span(q)]).astype(f32)
        wide = jnp.concatenate([head, x], axis=0)
        return x, wide[15:15 + rows], wide[14:14 + rows]

    def tap(c, j, q):
        return sk_ref[c, j:j + 1, span(q)]

    def short(c, n, q):
        x0, x1, x2 = delayed(c, n, q)
        return (tap(c, 0, q) * x0 + tap(c, 1, q) * x1 + tap(c, 2, q) * x2).astype(bf16)

    tail, lead = pl.ds(tokens, filt_len), pl.ds(0, filt_len)
    rims, grims, halos_later, halos_sooner = [], [], {}, {}
    for q in range(slabs):
        rims.append(remote(x_ref.at[pl.ds(0, 3), pl.ds(tokens - 16, 16), span(q)], rim.at[:, :, span(q)],
                           rim_send.at[q], rim_recv.at[q], later))
        grims.append(remote(gs.at[:, pl.ds(0, 8), span(q)], grim.at[:, :, span(q)],
                            rim_send.at[slabs + q], rim_recv.at[slabs + q], sooner))
        for i, ref in enumerate((vbuf, ibuf)):
            halos_later[q, i] = remote(ref.at[tail, span(q)], ref.at[lead, span(q)],
                                       halo_send.at[4 * q + i], halo_recv.at[4 * q + i], later)
        for i, ref in enumerate((gbuf, hbuf)):
            halos_sooner[q, i] = remote(ref.at[lead, span(q)], ref.at[tail, span(q)],
                                        halo_send.at[4 * q + 2 + i], halo_recv.at[4 * q + 2 + i], sooner)

    lane = lax.broadcasted_iota(jnp.int32, (rows, LANES), 1)

    def pair_span(p):
        return slice(p * LANES, (p + 1) * LANES)

    def pairs_in(q):
        return range(q * WIDTH // LANES, (q + 1) * WIDTH // LANES)

    def long(mats, k, src, n, q):
        parts = []
        for p in pairs_in(q):
            stacked = jnp.dot(mats[k, p], src[pl.ds(n * rows, window), pair_span(p)], preferred_element_type=f32)
            parts.append(jnp.where(lane < half, stacked[:rows], stacked[rows:]))
        return jnp.concatenate(parts, axis=1)

    flip_r = lax.broadcasted_iota(jnp.int32, (rows, rows), 0)
    flip_c = lax.broadcasted_iota(jnp.int32, (rows, rows), 1)
    flip = (flip_r + flip_c == rows - 1).astype(f32).astype(bf16)

    def scores(k, grad, src, p):
        total = None
        for n in range(count):
            turned = jnp.dot(flip, grad[pl.ds(n * rows, rows), pair_span(p)], preferred_element_type=f32)
            low = jnp.where(lane < half, turned, 0.0).astype(bf16)
            high = jnp.where(lane < half, 0.0, turned).astype(bf16)
            term = lax.dot_general(
                jnp.concatenate([low, high], axis=0), src[pl.ds(n * rows, window), pair_span(p)],
                (((1,), (1,)), ((), ())), preferred_element_type=f32)
            total = term if total is None else total + term
        score[...] = total
        for h in range(2):
            turned = pltpu.roll(score[pl.ds(h * rows, rows), :], 0, 1, stride=1, stride_axis=0)
            pfilt[z, pl.ds(k * heads + 2 * p + h, 1), :] = jnp.sum(turned, axis=0, keepdims=True)

    home, exits = {}, {}

    def send_back(i, q):
        def piece(k):
            there = pl.ds(pl.multiple_of(k * rows, rows), rows)
            return y_ref.at[pl.ds(1, 3), there, span(q)] if i else y_ref.at[0, there, span(q)]

        dst = grads_hbm.at[:, :, lanes_of(w, q)] if i else out_hbm.at[:, lanes_of(w, q)]
        for o, k in enumerate(partners):
            exits[q, i, o] = remote(piece(k), dst, back_send.at[2 * q + i, o], back_recv.at[2 * q + i, o], near(k))
            exits[q, i, o].start()
        home[q, i] = pltpu.make_async_copy(piece(w), dst, out_own.at[2 * q + i])
        home[q, i].start()

    def stage_enter(q):
        make_bands(q)
        arrived(q)
        if q + AHEAD < slabs:
            enter(q + AHEAD)
        to_later(rims[q])

    def stage_short(q):
        from_sooner(rims[q])
        for n in range(count):
            vbuf[pl.ds(filt_len + n * rows, rows), span(q)] = short(2, n, q)
        to_later(halos_later[q, 0])
        for n in range(count):
            here = pl.ds(n * rows, rows)
            gate = short(1, n, q)
            second[here, span(q)] = gate
            gbuf[here, span(q)] = (x_ref[3, here, span(q)].astype(f32) * gate.astype(f32)).astype(bf16)
        to_sooner(halos_sooner[q, 0])
        for n in range(count):
            first[pl.ds(n * rows, rows), span(q)] = short(0, n, q)

    def stage_inner(q):
        from_sooner(halos_later[q, 0])
        from_later(halos_sooner[q, 0])
        for n in range(count):
            here = pl.ds(n * rows, rows)
            gate = first[here, span(q)].astype(f32)
            one = long(bands, 0, vbuf, n, q)
            ibuf[pl.ds(filt_len + n * rows, rows), span(q)] = (gate * one).astype(bf16)
            back = long(adjs, 1, gbuf, n, q)
            gs[0, here, span(q)] = back * one
            hbuf[here, span(q)] = (back * gate).astype(bf16)
        to_later(halos_later[q, 1])
        to_sooner(halos_sooner[q, 1])

    def stage_outer(q):
        from_sooner(halos_later[q, 1])
        from_later(halos_sooner[q, 1])
        for n in range(count):
            here = pl.ds(n * rows, rows)
            two = long(bands, 1, ibuf, n, q)
            y_ref[0, here, span(q)] = (second[here, span(q)].astype(f32) * two).astype(bf16)
            gs[1, here, span(q)] = x_ref[3, here, span(q)].astype(f32) * two
            gs[2, here, span(q)] = long(adjs, 0, hbuf, n, q)
        to_sooner(grims[q])
        send_back(0, q)

    def stage_grads(q):
        from_later(grims[q])
        for c in range(3):
            for n in range(count):
                here = pl.ds(n * rows, rows)
                g = gs[c, here, span(q)]
                after = grim[c, :, span(q)] if n == count - 1 else gs[c, pl.ds((n + 1) * rows, 8), span(q)]
                wide = jnp.concatenate([g, after], axis=0)
                y_ref[1 + c, here, span(q)] = (
                    tap(c, 0, q) * g + tap(c, 1, q) * wide[1:1 + rows] + tap(c, 2, q) * wide[2:2 + rows]
                ).astype(bf16)
        send_back(1, q)

    def stage_sums(q):
        for p in pairs_in(q):
            scores(0, hbuf, vbuf, p)
            scores(1, gbuf, ibuf, p)
        for c in range(3):
            sums = [jnp.zeros((8, WIDTH), f32) for _ in range(3)]
            for n in range(count):
                g = gs[c, pl.ds(n * rows, rows), span(q)]
                for j, x in enumerate(delayed(c, n, q)):
                    sums[j] = sums[j] + jnp.sum((g * x).reshape(rows // 8, 8, WIDTH), axis=0)
            for j in range(3):
                pshort[z, pl.ds(3 * c + j, 1), span(q)] = jnp.sum(sums[j], axis=0, keepdims=True)

    pshort[z, pl.ds(9, 7), :] = jnp.zeros((7, chans), f32)
    for t in range(slabs + 3):
        for stage, q in ((stage_inner, t - 1), (stage_grads, t - 2), (stage_enter, t),
                         (stage_outer, t - 1), (stage_short, t), (stage_sums, t - 3)):
            if 0 <= q < slabs:
                stage(q)

    parts = []
    for o, k in enumerate(others):
        for i, ref in enumerate((pshort, pfilt)):
            copy = remote(ref.at[z], ref.at[z], part_send.at[i, o], part_recv.at[i, o], along(k))
            copy.start()
            parts.append(copy)
    for copy in parts:
        copy.wait_recv()
    total = float(rows * seq)
    fshort[w] = jnp.sum(pshort[...], axis=0) / jnp.sqrt(jnp.float32(total))
    ffilt[w] = jnp.sum(pfilt[...], axis=0) / jnp.sqrt(jnp.float32(total * half))
    fulls = []
    for o, k in enumerate(partners):
        for i, ref in enumerate((fshort, ffilt)):
            copy = remote(ref.at[w], ref.at[w], full_send.at[i, o], full_recv.at[i, o], near(k))
            copy.start()
            fulls.append(copy)
    for copy in fulls:
        copy.wait_recv()
    gshort_ref[...] = fshort[...]
    gfilt_ref[...] = ffilt[...]
    for copy in home.values():
        copy.wait()
    for copy in exits.values():
        copy.wait_recv()
    for copy in list(entry.values()) + list(exits.values()) + parts + fulls:
        copy.wait_send()
    if far > 1:
        for copy in rims + list(halos_later.values()):
            pl.when(has_later)(copy.wait_send)
        for copy in grims + list(halos_sooner.values()):
            pl.when(has_sooner)(copy.wait_send)


def on_device(streams, short_kernel, filters, cotangent):
    f32, bf16 = jnp.float32, jnp.bfloat16
    rows, width = streams.shape[1], streams.shape[2]
    seq = lax.axis_size("seq")
    filt_len = filters.shape[2]
    group = GROUP
    far = seq // group
    w = lax.rem(lax.axis_index("seq"), group)
    tokens, chans = rows * group, width // group
    heads = filters.shape[1] // group
    pairs = chans // LANES
    window = filt_len + rows
    sk = lax.dynamic_slice_in_dim(short_kernel, w * chans, chans, 2)
    taps = lax.dynamic_slice_in_dim(filters, w * heads, heads, 1).astype(bf16).astype(f32).reshape(2 * heads, filt_len)
    fwd = jnp.pad(taps[:, ::-1], ((0, 0), (1, rows - 1)))
    adj = jnp.pad(taps, ((0, 0), (0, rows)))
    hbm = pl.BlockSpec(memory_space=pltpu.HBM)
    vmem = pl.BlockSpec(memory_space=pltpu.VMEM)
    dma = pltpu.SemaphoreType.DMA
    output, grad_streams, gshort, gfilt = pl.pallas_call(
        functools.partial(hyena_kernel, rows, filt_len, seq, group),
        out_shape=(
            jax.ShapeDtypeStruct((rows, width), bf16),
            jax.ShapeDtypeStruct((3, rows, width), bf16),
            jax.ShapeDtypeStruct((group, 16, chans), f32),
            jax.ShapeDtypeStruct((group, 2 * heads, window), f32),
        ),
        in_specs=[hbm, hbm, vmem, vmem, vmem],
        out_specs=(hbm, hbm, vmem, vmem),
        scratch_shapes=[
            pltpu.VMEM((4, tokens, chans), bf16),
            pltpu.VMEM((4, tokens, chans), bf16),
            pltpu.VMEM((3, 16, chans), bf16),
            pltpu.VMEM((3, 8, chans), f32),
            pltpu.VMEM((2, pairs, 2 * rows, window), bf16),
            pltpu.VMEM((2, pairs, 2 * rows, window), bf16),
            pltpu.VMEM((tokens + filt_len, chans), bf16),
            pltpu.VMEM((tokens + filt_len, chans), bf16),
            pltpu.VMEM((tokens + filt_len, chans), bf16),
            pltpu.VMEM((tokens + filt_len, chans), bf16),
            pltpu.VMEM((tokens, chans), bf16),
            pltpu.VMEM((tokens, chans), bf16),
            pltpu.VMEM((2 * rows, window), f32),
            pltpu.VMEM((3, tokens, chans), f32),
            pltpu.VMEM((far, 16, chans), f32),
            pltpu.VMEM((far, 2 * heads, window), f32),
            pltpu.VMEM((group, 16, chans), f32),
            pltpu.VMEM((group, 2 * heads, window), f32),
            dma((2 * pairs,)),
            dma((2 * pairs, group - 1)),
            dma((2 * pairs, group - 1)),
            dma((2 * pairs, group - 1)),
            dma((2 * pairs, group - 1)),
            dma((2 * pairs,)),
            dma((2 * pairs,)),
            dma((2 * pairs,)),
            dma((4 * pairs,)),
            dma((4 * pairs,)),
            dma((2, max(far - 1, 1))),
            dma((2, max(far - 1, 1))),
            dma((2, group - 1)),
            dma((2, group - 1)),
        ],
        compiler_params=pltpu.CompilerParams(
            vmem_limit_bytes=48 * 1024 * 1024, collective_id=0, has_side_effects=True),
    )(streams, cotangent, sk, fwd, adj)
    grad_short = gshort[:, :9].reshape(group, 3, 3, chans).transpose(1, 2, 0, 3).reshape(3, 3, width)
    gfilt = gfilt[:, :, rows:][:, :, ::-1].reshape(group, 2, heads, filt_len)
    grad_filters = gfilt.transpose(1, 0, 2, 3).reshape(2, group * heads, filt_len)
    return (output, grad_streams, grad_short, grad_filters)


def solution(mesh):
    placed = (P(None, ("groups", "seq"), None), P(), P(), P(("groups", "seq"), None))
    return jax.shard_map(
        on_device,
        mesh=mesh,
        in_specs=placed,
        out_specs=(
            P(("groups", "seq"), None),
            P(None, ("groups", "seq"), None),
            P("groups", None, None),
            P("groups", None, None),
        ),
        check_vma=False,
    )
```
